256 devices in a mesh: dp: 4 (over x), depth: 2 (over y_hi), tensor: 32 (over y_lo, z, core).
Axes of the slice: x: 4, y: 4 (y_hi: 2, y_lo: 2; y = y_hi * 2 + y_lo), z: 8, core: 2. Of those that a mesh axis runs over, the one named last changes fastest.
Arguments:
- text: bfloat16 [512, 8192], P(('dp', 'tensor')), may hold values from -6 to 6
- vision: bfloat16 [1024, 8192], P(('dp', 'depth'), 'tensor'), may hold values from -6 to 6
- query_weight: bfloat16 [2, 8192, 8192], P('depth', None, 'tensor'), may hold values from -0.0625 to 0.0625
- key_weight: bfloat16 [2, 8192, 1024], P('depth', 'tensor'), may hold values from -0.0625 to 0.0625
- value_weight: bfloat16 [2, 8192, 1024], P('depth', 'tensor'), may hold values from -0.0625 to 0.0625
- out_weight: bfloat16 [2, 8192, 8192], P('depth', 'tensor'), may hold values from -0.25 to 0.25
- gate: float32 [2], P('depth'), may hold values from 0.5 to 1.5
- cotangent: bfloat16 [512, 8192], P(('dp', 'tensor')), may hold values from -0.75 to 0.75
- tile_table: int32 [4, 8, 4], P('dp'), may hold values 0 or 1
- vision_tiles: int32 [4], P('dp'), may hold values from 1 to 4
- text_lengths: int32 [4], P('dp'), may hold values from 64 to 128
Outputs:
- hidden_states: bfloat16 [2, 512, 8192], P('depth', ('dp', 'tensor'))
- text_grads: bfloat16 [2, 512, 8192], P('depth', ('dp', 'tensor'))
- vision_grad: float32 [1024, 8192], P(('dp', 'depth'), 'tensor')
- key_weight_grad: float32 [2, 8192, 1024], P('depth', 'tensor', 'dp')
- value_weight_grad: float32 [2, 8192, 1024], P('depth', 'tensor', 'dp')
The draws below stay inside these ranges and needn't reach their ends.
All inputs are finite; a program needn't handle non-finite values. No bound on the sum of `tile_table` on one device may be relied on, other than what follows from the above.
Results may differ from the reference program's by a relative error of at most 0.034.
Values may be sent and summed in bfloat16 or wider, within the bound.
No kernel may reach another device: no remote copies, remote signals or barrier semaphores. Data moves between devices by JAX's collectives and lax.ppermute only.
A program may use at most 128 MiB of HBM per device.

```python
import math
import jax
import jax.numpy as jnp
from jax import lax

D = 8192
HD = 128
HEAD_DEV = 2
QGROUP = 8
SEQ = 128
TBLK = 16
TILES = 4
TILE_ROWS = 64
LAYERS = 2
HEADS = 64
KVH = 8
VIS = 256
N_DP = 4
N_TENSOR = 32


def plant(values, rng, smallest, top_value):
    shape = values.shape
    place = [jax.random.randint(jax.random.fold_in(rng, axis), (), 0, shape[axis]) for axis in range(len(shape))]
    values = values.at[tuple(place)].set(smallest)
    longest = shape.index(max(shape))
    place[longest] = (place[longest] + 1) % shape[longest]
    return values.at[tuple(place)].set(top_value)


def level_of(stream_key, extent, cuts, least, largest):
    def one(axis_at, parts):
        steps = jax.random.uniform(jax.random.fold_in(jax.random.fold_in(stream_key, 6), axis_at), (parts,), jnp.float32, least / len(cuts), largest / len(cuts))
        return jnp.repeat(jnp.exp(steps), extent[axis_at] // parts).reshape((-1,) + (1,) * (len(extent) - axis_at - 1))

    gain = one(*cuts[0])
    for cut in cuts[1:]:
        gain = gain * one(*cut)
    return gain


def gaussian(key, shape, deviation, limit, pieces=(), held_as=jnp.bfloat16):
    loudness = level_of(key, shape, pieces, -0.22, 0.18) if pieces else 1.0
    result = jax.random.normal(key, shape, jnp.float32) * deviation * loudness
    return jnp.minimum(jnp.maximum(result, -limit), limit).astype(held_as)


def setup_inputs(seed: int = 0) -> dict:
    splits = jax.random.split(jax.random.key(seed), 12)
    text = gaussian(splits[0], (N_DP * SEQ, D), 1.0, 6.0, ((0, 128),))
    vision = gaussian(splits[1], (N_DP * VIS, D), 1.0, 6.0, ((0, 8), (1, 32)))
    query_weight = gaussian(splits[2], (LAYERS, D, HEADS * HD), D ** -0.5, 0.0625, ((0, 2), (2, 32)))
    key_weight = gaussian(splits[3], (LAYERS, D, KVH * HD), D ** -0.5, 0.0625, ((0, 2), (1, 32)))
    value_weight = gaussian(splits[4], (LAYERS, D, KVH * HD), D ** -0.5, 0.0625, ((0, 2), (1, 32)))
    out_weight = gaussian(splits[5], (LAYERS, HEADS * HD, D), (4 * HD) ** -0.5, 0.25, ((0, 2), (1, 32)))
    gate = jnp.clip(0.5 + 1.0 * jax.random.uniform(splits[6], (LAYERS,), jnp.float32) ** level_of(splits[6], (LAYERS,), ((0, 2),), -0.2, 0.2), 0.5, 1.5)
    cotangent = gaussian(splits[7], (N_DP * SEQ, D), 0.125, 0.75, ((0, 128),))
    tile_table = plant((jax.random.randint(splits[8], (N_DP, SEQ // TBLK, TILES), 0, 3) < 2).astype(jnp.int32), jax.random.fold_in(splits[8], 1), 0, 1)
    vision_tiles = plant(jax.random.randint(splits[9], (N_DP,), 1, TILES + 1), jax.random.fold_in(splits[9], 1), 1, TILES).astype(jnp.int32)
    text_lengths = plant(jax.random.randint(splits[10], (N_DP,), SEQ // 2, SEQ + 1), jax.random.fold_in(splits[10], 1), SEQ // 2, SEQ).astype(jnp.int32)
    return dict(text=text, vision=vision, query_weight=query_weight, key_weight=key_weight, value_weight=value_weight, out_weight=out_weight, gate=gate, cotangent=cotangent, tile_table=tile_table, vision_tiles=vision_tiles, text_lengths=text_lengths)


def normalize(values, epsilon):
    return values * lax.rsqrt(lax.optimization_barrier(jnp.mean(values * values, axis=-1, keepdims=True)) + epsilon)

def norm_back(values, upstream, epsilon):
    inv_rms = lax.rsqrt(lax.optimization_barrier(jnp.mean(values * values, axis=-1, keepdims=True)) + epsilon)
    normed = values * inv_rms
    return inv_rms * (upstream - normed * lax.optimization_barrier(jnp.mean(upstream * normed, axis=-1, keepdims=True)))

def allowed_mask(table, tile_count, text_count):
    tile_ok = jnp.arange(TILES, dtype=jnp.int32) < tile_count
    block_ok = (table > 0) & tile_ok[None, :]
    full_mask = jnp.broadcast_to(block_ok[:, None, :, None], (SEQ // TBLK, TBLK, TILES, TILE_ROWS)).reshape(SEQ, VIS)
    row_ok = jnp.arange(SEQ, dtype=jnp.int32) < text_count
    return full_mask & row_ok[:, None]

def reference(text, vision, query_weight, key_weight, value_weight, out_weight, gate, cotangent, tile_table, vision_tiles, text_lengths):
    groups = N_TENSOR
    local_width = HEAD_DEV * HD
    inv_sqrt = 1.0 / math.sqrt(HD)
    hidden_all = [[] for layer_at in range(LAYERS)]
    grads_all = [[] for layer_at in range(LAYERS)]
    vision_all = []
    dkey_total = jnp.zeros((LAYERS, D, KVH * HD), jnp.float32)
    dvalue_total = jnp.zeros((LAYERS, D, KVH * HD), jnp.float32)
    for sample in range(N_DP):
        inputs = text[sample * SEQ:(sample + 1) * SEQ]
        vis_rows = vision[sample * VIS:(sample + 1) * VIS]
        allowed = allowed_mask(tile_table[sample], vision_tiles[sample], text_lengths[sample])
        row_live = jnp.any(allowed, axis=-1).astype(jnp.float32)
        kept_all = []
        for layer_at in range(LAYERS):
            key_pre = jnp.dot(vis_rows, key_weight[layer_at], preferred_element_type=jnp.float32).reshape(VIS, KVH, HD)
            key_cast = normalize(key_pre, 1e-06).astype(jnp.bfloat16)
            value_cast = jnp.dot(vis_rows, value_weight[layer_at], preferred_element_type=jnp.float32).astype(jnp.bfloat16).reshape(VIS, KVH, HD)
            inputs_f = inputs.astype(jnp.float32)
            normed = normalize(inputs_f, 1e-05).astype(jnp.bfloat16)
            query = jnp.dot(normed, query_weight[layer_at], preferred_element_type=jnp.float32).reshape(SEQ, KVH, QGROUP, HD)
            query_cast = normalize(query, 1e-06).astype(jnp.bfloat16)
            scores = jnp.einsum('sgqd,vgd->gqsv', query_cast.astype(jnp.float32), key_cast.astype(jnp.float32)) * inv_sqrt
            expd = jnp.where(allowed, jnp.exp(scores), 0.0)
            probs = expd / (lax.optimization_barrier(jnp.sum(expd, axis=-1, keepdims=True)) + (1.0 - row_live)[:, None])
            probs_cast = probs.astype(jnp.bfloat16)
            mixed = jnp.einsum('gqsv,vgd->sgqd', probs_cast.astype(jnp.float32), value_cast.astype(jnp.float32)).astype(jnp.bfloat16)
            mixed_groups = mixed.reshape(SEQ, groups, local_width).astype(jnp.float32)
            out_groups = out_weight[layer_at].reshape(groups, local_width, D).astype(jnp.float32)
            terms = jnp.einsum('sgk,gkd->gsd', mixed_groups, out_groups).astype(jnp.bfloat16)
            attended = lax.optimization_barrier(jnp.sum(terms.astype(jnp.float32), axis=0))
            gate_value = jnp.tanh(gate[layer_at])
            outputs = (inputs_f + gate_value * attended).astype(jnp.bfloat16)
            kept_all.append((inputs, key_pre, key_cast, value_cast, query, query_cast, probs, probs_cast))
            hidden_all[layer_at].append(outputs)
            inputs = outputs
        upstream = cotangent[sample * SEQ:(sample + 1) * SEQ]
        vision_grad = jnp.zeros((VIS, D), jnp.float32)
        for layer_at in reversed(range(LAYERS)):
            inputs, key_pre, key_cast, value_cast, query, query_cast, probs, probs_cast = kept_all[layer_at]
            gate_value = jnp.tanh(gate[layer_at])
            scaled = (gate_value * upstream.astype(jnp.float32)).astype(jnp.bfloat16)
            dmixed = jnp.dot(scaled, out_weight[layer_at].T, preferred_element_type=jnp.float32).astype(jnp.bfloat16).reshape(SEQ, KVH, QGROUP, HD)
            dprobs = jnp.einsum('sgqd,vgd->gqsv', dmixed.astype(jnp.float32), value_cast.astype(jnp.float32))
            dvalue = jnp.einsum('gqsv,sgqd->vgd', probs_cast.astype(jnp.float32), dmixed.astype(jnp.float32))
            dscores = (probs * (dprobs - lax.optimization_barrier(jnp.sum(probs * dprobs, axis=-1, keepdims=True))) * inv_sqrt).astype(jnp.bfloat16)
            dquery_hat = jnp.einsum('gqsv,vgd->sgqd', dscores.astype(jnp.float32), key_cast.astype(jnp.float32))
            dkey_hat = jnp.einsum('gqsv,sgqd->vgd', dscores.astype(jnp.float32), query_cast.astype(jnp.float32))
            dquery = norm_back(query, dquery_hat, 1e-06).astype(jnp.bfloat16).reshape(SEQ, groups, local_width)
            query_groups = query_weight[layer_at].reshape(D, groups, local_width).astype(jnp.float32)
            terms = jnp.einsum('sgk,dgk->gsd', dquery.astype(jnp.float32), query_groups).astype(jnp.bfloat16)
            dnormed = lax.optimization_barrier(jnp.sum(terms.astype(jnp.float32), axis=0))
            dinputs = (upstream.astype(jnp.float32) + norm_back(inputs.astype(jnp.float32), dnormed, 1e-05)).astype(jnp.bfloat16)
            dkey_pre = norm_back(key_pre, dkey_hat, 1e-06).astype(jnp.bfloat16).reshape(VIS, KVH * HD)
            dvalue_cast = dvalue.astype(jnp.bfloat16).reshape(VIS, KVH * HD)
            vision_grad = vision_grad + jnp.dot(dkey_pre, key_weight[layer_at].T, preferred_element_type=jnp.float32) + jnp.dot(dvalue_cast, value_weight[layer_at].T, preferred_element_type=jnp.float32)
            dkey_total = dkey_total.at[layer_at].add(jnp.dot(vis_rows.T, dkey_pre, preferred_element_type=jnp.float32))
            dvalue_total = dvalue_total.at[layer_at].add(jnp.dot(vis_rows.T, dvalue_cast, preferred_element_type=jnp.float32))
            grads_all[layer_at].append(dinputs)
            upstream = dinputs
        vision_all.append(vision_grad)
    hidden_states = jnp.stack([jnp.concatenate(hidden_all[layer_at], axis=0) for layer_at in range(LAYERS)])
    text_grads = jnp.stack([jnp.concatenate(grads_all[layer_at], axis=0) for layer_at in range(LAYERS)])
    return (hidden_states, text_grads, jnp.concatenate(vision_all, axis=0), dkey_total, dvalue_total)
```

```python
import math

import jax
import jax.numpy as jnp
import numpy as np
from jax import lax
from jax.experimental import pallas as pl
from jax.sharding import PartitionSpec as P

HD = 128
QGROUP = 8
SEQ = 128
TBLK = 16
TILES = 4
TILE_ROWS = 64
VIS = 256
NT = 32
NZ = 8
INV_SQRT = 1.0 / math.sqrt(HD)
BF = jnp.bfloat16
F32 = jnp.float32


def split_index(t):
    return t // 16, (t // 2) % NZ, t % 2


def join_index(y, z, c):
    return (y % 2) * 16 + (z % NZ) * 2 + (c % 2)


def moved(move):
    return [(t, join_index(*move(*split_index(t)))) for t in range(NT)]


TO_CORE = moved(lambda y, z, c: (y, z, c + 1))
TO_ROW = moved(lambda y, z, c: (y + 1, z, c))
TO_BOTH = moved(lambda y, z, c: (y + 1, z, c + 1))
RING = moved(lambda y, z, c: (y, z + 1 if c == 0 else z - 1, c))
KV_PAIR = moved(lambda y, z, c: (y, z ^ 1, c))
KV_BOTH = moved(lambda y, z, c: (y, z ^ 1, c + 1))
Z_GROUPS = [[join_index(y, z, c) for z in range(NZ)] for y in range(2) for c in range(2)]


def gathered_owners():
    table = np.zeros((NT, NT), np.int32)
    for t in range(NT):
        y, z, c = split_index(t)

        def chip(at, core):
            return [
                join_index(y, at, core),
                join_index(y, at, core + 1),
                join_index(y + 1, at, core),
                join_index(y + 1, at, core + 1),
            ]

        def received(core, step):
            at = z - step if core == 0 else z + step
            held = chip(at, core)
            if step < 4:
                return held
            return held[:2] if core == 0 else held[2:]

        order = chip(z, c)
        for step in range(1, 5):
            order += received(c, step) + received(1 - c, step)
        table[t] = order
    return table


OWNERS = gathered_owners()


def summed_owners():
    table = np.zeros((NT, NT), np.int32)
    for t in range(NT):
        y, _, c = split_index(t)
        table[t] = [
            join_index(y + dy, z, c + dc) for dc in (1, 0) for dy in (1, 0) for z in range(NZ)
        ]
    return table


TARGETS = summed_owners()


def hop(value, pairs):
    return lax.ppermute(value, "tensor", pairs)


def gather_rows(shard, core):
    rows = shard.shape[0]
    chip = jnp.concatenate(
        [shard, hop(shard, TO_CORE), hop(shard, TO_ROW), hop(shard, TO_BOTH)], axis=0
    )
    parts = [chip]
    held = chip
    for step in range(1, 5):
        if step == 4:
            held = jnp.where(core == 0, held[: 2 * rows], held[2 * rows :])
        held = hop(held, RING)
        parts += [held, hop(held, TO_CORE)]
    return parts


def z_exchange(value):
    return lax.all_to_all(value, "tensor", 0, 0, axis_index_groups=Z_GROUPS)


def token_sums(product, rows):
    half, quarter = SEQ // 2, SEQ // 4
    away = product(rows[:half]).astype(BF)
    arrived = hop(away, TO_CORE)
    pair = product(rows[half:]) + arrived.astype(F32)
    arrived = hop(pair[:quarter].astype(BF), TO_ROW)
    quad = (pair[quarter:] + arrived.astype(F32)).astype(BF)
    pieces = z_exchange(quad.reshape(NZ, quarter // NZ, quad.shape[1]))
    return jnp.sum(pieces.astype(F32), axis=0)


def normalize(values, epsilon):
    return values * lax.rsqrt(jnp.mean(values * values, axis=-1, keepdims=True) + epsilon)


def norm_back(values, upstream, epsilon):
    inv_rms = lax.rsqrt(jnp.mean(values * values, axis=-1, keepdims=True) + epsilon)
    normed = values * inv_rms
    return inv_rms * (upstream - normed * jnp.mean(upstream * normed, axis=-1, keepdims=True))


def dot_nt(a, b):
    return lax.dot_general(a, b, (((1,), (1,)), ((), ())), preferred_element_type=F32)


def dot_tn(a, b):
    return lax.dot_general(a, b, (((0,), (0,)), ((), ())), preferred_element_type=F32)


def dot_nn(a, b):
    return lax.dot_general(a, b, (((1,), (0,)), ((), ())), preferred_element_type=F32)


def head_probs(query, keys, allowed):
    query_cast = normalize(query, 1e-06).astype(BF)
    scores = dot_nt(query_cast, keys) * INV_SQRT
    expd = jnp.where(allowed > 0.0, jnp.exp(scores), 0.0)
    live = jnp.max(allowed, axis=-1, keepdims=True)
    probs = expd / (jnp.sum(expd, axis=-1, keepdims=True) + (1.0 - live))
    return query_cast, probs


def forward_kernel(query_ref, keys_ref, values_ref, allowed_ref, order_ref, mixed_ref):
    keys = keys_ref[...]
    values = values_ref[...]
    allowed = allowed_ref[...]
    order = order_ref[...]
    for at in range(0, query_ref.shape[1], HD):
        _, probs = head_probs(query_ref[:, at : at + HD], keys, allowed)
        mixed = dot_nn(probs.astype(BF), values).astype(BF)
        mixed_ref[:, at : at + HD] = dot_nn(order, mixed).astype(BF)


def backward_kernel(
    query_ref,
    dmixed_ref,
    keys_ref,
    values_ref,
    allowed_ref,
    order_ref,
    dquery_ref,
    dkeys_ref,
    dvalues_ref,
):
    keys = keys_ref[...]
    values = values_ref[...]
    allowed = allowed_ref[...]
    order = order_ref[...]
    dkeys = 0.0
    dvalues = 0.0
    for at in range(0, query_ref.shape[1], HD):
        query = query_ref[:, at : at + HD]
        query_cast, probs = head_probs(query, keys, allowed)
        dmixed = dmixed_ref[:, at : at + HD].astype(BF)
        dprobs = dot_nt(dmixed, values)
        dvalues += dot_tn(probs.astype(BF), dmixed)
        dscores = (
            probs * (dprobs - jnp.sum(probs * dprobs, axis=-1, keepdims=True)) * INV_SQRT
        ).astype(BF)
        dkeys += dot_tn(dscores, query_cast)
        dquery = norm_back(query, dot_nn(dscores, keys), 1e-06).astype(BF)
        dquery_ref[:, at : at + HD] = dot_nn(order, dquery).astype(BF)
    dkeys_ref[...] = dkeys
    dvalues_ref[...] = dvalues


def attend(query, keys, values, allowed, order):
    return pl.pallas_call(
        forward_kernel,
        out_shape=jax.ShapeDtypeStruct(query.shape, BF),
        name="attend",
    )(query, keys, values, allowed, order)


def attend_back(query, dmixed, keys, values, allowed, order):
    return pl.pallas_call(
        backward_kernel,
        out_shape=(
            jax.ShapeDtypeStruct(query.shape, BF),
            jax.ShapeDtypeStruct(keys.shape, F32),
            jax.ShapeDtypeStruct(values.shape, F32),
        ),
        name="attend_back",
    )(query, dmixed, keys, values, allowed, order)


def owned_rows(owners):
    return jnp.repeat(owners * (SEQ // NT), SEQ // NT) + jnp.tile(
        jnp.arange(SEQ // NT, dtype=jnp.int32), NT
    )


def place_pieces(parts, owners):
    rows = TILE_ROWS

    def kernel(owners_ref, *refs):
        ins, (keys_ref, values_ref) = refs[:-2], refs[-2:]
        at = 0
        for ref in ins:
            for first in range(0, ref.shape[0], rows):
                owner = owners_ref[at]
                place = pl.ds(pl.multiple_of((owner % 4) * rows, rows), rows)
                piece = ref[first : first + rows, :]
                keys_ref[owner // 4, place, :] = piece[:, :HD]
                values_ref[owner // 4, place, :] = piece[:, HD:]
                at += 1

    from jax.experimental.pallas import tpu as pltpu

    shape = jax.ShapeDtypeStruct((NT // 4, VIS, HD), BF)
    return pl.pallas_call(
        kernel,
        out_shape=(shape, shape),
        in_specs=[pl.BlockSpec(memory_space=pltpu.SMEM)]
        + [pl.BlockSpec(memory_space=pltpu.VMEM)] * len(parts),
        name="place_pieces",
    )(owners, *parts)


def per_device(
    text,
    vision,
    query_weight,
    key_weight,
    value_weight,
    out_weight,
    gate,
    cotangent,
    tile_table,
    vision_tiles,
    text_lengths,
):
    section = lax.axis_index("depth")
    first = section == 0
    tensor = lax.axis_index("tensor")
    row = tensor // 16
    core = tensor % 2
    tile = tensor % 4
    w_query = query_weight[0]
    w_key = key_weight[0]
    w_value = value_weight[0]
    w_out = out_weight[0]
    gate_value = jnp.tanh(gate[0])
    depth_swap = [(0, 1), (1, 0)]

    owners = lax.dynamic_index_in_dim(jnp.asarray(OWNERS), tensor, 0, False)
    targets = lax.dynamic_index_in_dim(jnp.asarray(TARGETS), tensor, 0, False)
    row_at = owned_rows(owners)
    order = (owned_rows(targets)[:, None] == row_at[None, :]).astype(BF)

    tile_ok = jnp.arange(TILES, dtype=jnp.int32) < vision_tiles[0]
    block_ok = ((tile_table[0] > 0) & tile_ok[None, :]).astype(F32)
    column_tile = jnp.bitwise_xor(tile, jnp.arange(VIS, dtype=jnp.int32) // TILE_ROWS)
    row_block = row_at // TBLK
    allowed = jnp.zeros((SEQ, VIS), F32)
    for at in range(TILES):
        hit = jnp.zeros((SEQ,), F32)
        for block in range(SEQ // TBLK):
            hit = hit + jnp.where(row_block == block, block_ok[block, at], 0.0)
        hit = jnp.where(row_at < text_lengths[0], hit, 0.0)
        allowed = allowed + jnp.where(column_tile == at, 1.0, 0.0)[None, :] * hit[:, None]

    text_f = text.astype(F32)
    cotangent_f = cotangent.astype(F32)

    opening = jnp.where(first, normalize(text_f, 1e-05), gate_value * cotangent_f).astype(BF)
    opened = jnp.concatenate(gather_rows(opening, core), axis=0)

    other = lax.ppermute(vision, "depth", depth_swap)
    low = jnp.where(first, vision, other)
    high = jnp.where(first, other, vision)
    tiles = [low[:TILE_ROWS], low[TILE_ROWS:], high[:TILE_ROWS], high[TILE_ROWS:]]
    even = jnp.concatenate([tiles[0], tiles[2]], axis=0)
    odd = jnp.concatenate([tiles[1], tiles[3]], axis=0)
    near = jnp.where(core == 0, even, odd)
    far = jnp.where(core == 0, odd, even)
    away = jnp.concatenate([dot_nn(far, w_key).astype(BF), dot_nn(far, w_value).astype(BF)], axis=1)
    arrived = hop(away, TO_CORE).astype(F32)
    kv_width = w_key.shape[1]
    width = kv_width // 2
    keys_half = dot_nn(near, w_key) + arrived[:, :kv_width]
    values_half = dot_nn(near, w_value) + arrived[:, kv_width:]

    def columns(values, at):
        return lax.dynamic_slice_in_dim(values, at * width, width, 1)

    away = jnp.concatenate([columns(keys_half, 1 - row), columns(values_half, 1 - row)], axis=1)
    arrived = hop(away.astype(BF), TO_ROW).astype(F32)
    keys_quad = (columns(keys_half, row) + arrived[:, :width]).astype(BF)
    values_quad = (columns(values_half, row) + arrived[:, width:]).astype(BF)
    blocks = []
    for head in range(0, width, HD):
        for start in (0, TILE_ROWS):
            rows = slice(start, start + TILE_ROWS)
            lanes = slice(head, head + HD)
            blocks.append(
                jnp.concatenate([keys_quad[rows, lanes], values_quad[rows, lanes]], axis=1)
            )
    piece = jnp.sum(z_exchange(jnp.stack(blocks)).astype(F32), axis=0)
    keys_piece = piece[:, :HD]
    kv_piece = jnp.concatenate([normalize(keys_piece, 1e-06), piece[:, HD:]], axis=1).astype(BF)
    head_kv = jnp.concatenate(
        [kv_piece, hop(kv_piece, TO_CORE), hop(kv_piece, KV_PAIR), hop(kv_piece, KV_BOTH)], axis=0
    )
    keys = head_kv[:, :HD]
    values = head_kv[:, HD:]

    def out_product(rows):
        return dot_nn(rows, w_out)

    def in_product(rows):
        return dot_nt(rows, w_query)

    query_first = dot_nn(opened, w_query)
    dmixed_second = dot_nt(opened, w_out)
    mixed_first = attend(query_first, keys, values, allowed, order)
    attended = token_sums(out_product, mixed_first)
    hidden_first = (text_f + gate_value * attended).astype(BF)

    passed = lax.ppermute(hidden_first, "depth", [(0, 1)])
    passed_f = passed.astype(F32)
    middle = gather_rows(normalize(passed_f, 1e-05).astype(BF), core)
    query_second = dot_nn(jnp.concatenate(middle, axis=0), w_query)
    dquery_second, dkeys_second, dvalues_second = attend_back(
        query_second, dmixed_second, keys, values, allowed, order
    )
    dnormed = token_sums(in_product, dquery_second)
    grad_second = (cotangent_f + norm_back(passed_f, dnormed, 1e-05)).astype(BF)
    mixed_second = attend(query_second, keys, values, allowed, order)

    upstream = lax.ppermute(grad_second, "depth", [(1, 0)])
    upstream_f = upstream.astype(F32)
    closing = gather_rows((gate_value * upstream_f).astype(BF), core)
    dmixed_first = dot_nt(jnp.concatenate(closing, axis=0), w_out)
    dquery_first, dkeys_first, dvalues_first = attend_back(
        query_first, dmixed_first, keys, values, allowed, order
    )

    def last_product(rows):
        return lax.cond(first, in_product, out_product, rows)

    last_rows = jnp.where(first, dquery_first, mixed_second)
    last = token_sums(last_product, last_rows)
    grad_first = (upstream_f + norm_back(text_f, last, 1e-05)).astype(BF)
    hidden_second = (passed_f + gate_value * last).astype(BF)
    hidden = jnp.where(first, hidden_first, hidden_second)
    text_grad = jnp.where(first, grad_first, grad_second)

    dkv = jnp.concatenate(
        [
            jnp.where(first, dkeys_first, dkeys_second),
            jnp.where(first, dvalues_first, dvalues_second),
        ],
        axis=1,
    )
    dkv_piece = (
        dkv[:TILE_ROWS]
        + hop(dkv[TILE_ROWS : 2 * TILE_ROWS], TO_CORE)
        + hop(dkv[2 * TILE_ROWS : 3 * TILE_ROWS], KV_PAIR)
        + hop(dkv[3 * TILE_ROWS :], KV_BOTH)
    )
    dkv_piece = jnp.concatenate(
        [norm_back(keys_piece, dkv_piece[:, :HD], 1e-06), dkv_piece[:, HD:]], axis=1
    ).astype(BF)
    dkeys_all, dvalues_all = place_pieces(gather_rows(dkv_piece, core), owners)
    heads = NT // 4
    vis_full = jnp.concatenate([low, high], axis=0)
    weight_heads = w_key.reshape(w_key.shape[0], heads, HD)
    value_heads = w_value.reshape(w_value.shape[0], heads, HD)
    dvision = jnp.einsum(
        "hvc,dhc->vd", dkeys_all, weight_heads, preferred_element_type=F32
    ) + jnp.einsum("hvc,dhc->vd", dvalues_all, value_heads, preferred_element_type=F32)
    mine = lax.dynamic_slice_in_dim(dvision, section * (VIS // 2), VIS // 2, 0)
    theirs = lax.dynamic_slice_in_dim(dvision, (1 - section) * (VIS // 2), VIS // 2, 0)
    dvision = mine + lax.ppermute(theirs, "depth", depth_swap)

    samples = lax.axis_size("dp")
    vis_all = lax.all_gather(vis_full, "dp", axis=0, tiled=False)
    grouped = jnp.stack(
        [
            dkeys_all.reshape(samples, heads // samples, VIS, HD),
            dvalues_all.reshape(samples, heads // samples, VIS, HD),
        ],
        axis=1,
    )
    grouped = lax.all_to_all(grouped, "dp", 0, 0)
    dweights = jnp.einsum("svd,skhvc->kdhc", vis_all, grouped, preferred_element_type=F32)
    dweights = dweights.reshape(2, dweights.shape[1], -1)
    return (hidden[None], text_grad[None], dvision, dweights[0][None], dweights[1][None])


def solution(mesh):
    in_specs = (
        P(("dp", "tensor"), None),
        P(("dp", "depth"), "tensor"),
        P("depth", None, "tensor"),
        P("depth", "tensor", None),
        P("depth", "tensor", None),
        P("depth", "tensor", None),
        P("depth"),
        P(("dp", "tensor"), None),
        P("dp", None, None),
        P("dp"),
        P("dp"),
    )
    out_specs = (
        P("depth", ("dp", "tensor"), None),
        P("depth", ("dp", "tensor"), None),
        P(("dp", "depth"), "tensor"),
        P("depth", "tensor", "dp"),
        P("depth", "tensor", "dp"),
    )
    return jax.shard_map(
        per_device, mesh=mesh, in_specs=in_specs, out_specs=out_specs, check_vma=False
    )
```

```python
import math

import jax
import jax.numpy as jnp
from jax import lax
from jax.experimental import pallas as pl
from jax.experimental.pallas import tpu as pltpu
from jax.sharding import PartitionSpec as P

HD = 128
SEQ = 128
TBLK = 16
TILES = 4
TILE_ROWS = 64
VIS = 256
NT = 32
INV_SQRT = 1.0 / math.sqrt(HD)
BF = jnp.bfloat16
F32 = jnp.float32


def moved(move):
    pairs = []
    for t in range(NT):
        y, z, c = move(t // 16, (t // 2) % 8, t % 2)
        pairs.append((t, y * 16 + z * 2 + c))
    return pairs


TO_CORE = moved(lambda y, z, c: (y, z, 1 - c))
TO_ROW = moved(lambda y, z, c: (1 - y, z, c))
KV_PAIR = moved(lambda y, z, c: (y, z ^ 1, c))
KV_BOTH = moved(lambda y, z, c: (y, z ^ 1, 1 - c))
CHIPS = NT // 2
CHIP_GROUPS = [[2 * chip + c for chip in range(CHIPS)] for c in range(2)]
RING = 8
RING_GROUPS = [[16 * y + 2 * z + c for z in range(RING)] for y in range(2) for c in range(2)]
ROWS = SEQ // NT
HALF = SEQ // 2


def hop(value, pairs):
    return lax.ppermute(value, "tensor", pairs)


def chip_exchange(value):
    return lax.all_to_all(value, "tensor", 0, 0, axis_index_groups=CHIP_GROUPS)


def ring_exchange(value):
    return lax.all_to_all(value, "tensor", 0, 0, axis_index_groups=RING_GROUPS)


def after(value, earlier):
    return lax.optimization_barrier((value, earlier))[0]


def gather_chips(shard):
    near = chip_exchange(jnp.broadcast_to(shard[None], (CHIPS,) + shard.shape))
    return near, hop(near, TO_CORE)


def normalize(values, epsilon):
    return values * lax.rsqrt(jnp.mean(values * values, axis=-1, keepdims=True) + epsilon)


def norm_back(values, upstream, epsilon):
    inv_rms = lax.rsqrt(jnp.mean(values * values, axis=-1, keepdims=True) + epsilon)
    normed = values * inv_rms
    return inv_rms * (upstream - normed * jnp.mean(upstream * normed, axis=-1, keepdims=True))


def dot_nt(a, b):
    return lax.dot_general(a, b, (((1,), (1,)), ((), ())), preferred_element_type=F32)


def dot_tn(a, b):
    return lax.dot_general(a, b, (((0,), (0,)), ((), ())), preferred_element_type=F32)


def dot_nn(a, b):
    return lax.dot_general(a, b, (((1,), (0,)), ((), ())), preferred_element_type=F32)


def head_probs(query, keys, allowed):
    query_cast = normalize(query, 1e-06).astype(BF)
    scores = dot_nt(query_cast, keys) * INV_SQRT
    expd = jnp.where(allowed > 0.0, jnp.exp(scores), 0.0)
    live = jnp.max(allowed, axis=-1, keepdims=True)
    probs = expd / (jnp.sum(expd, axis=-1, keepdims=True) + (1.0 - live))
    return query_cast, probs


def local_call(kernel, outs, ins, name, scratch=()):
    held = pl.BlockSpec(memory_space=pltpu.VMEM)
    return pl.pallas_call(
        kernel,
        in_specs=[held] * len(ins),
        out_specs=[held] * len(outs),
        out_shape=[jax.ShapeDtypeStruct(shape, dtype) for shape, dtype in outs],
        scratch_shapes=list(scratch),
        compiler_params=pltpu.CompilerParams(vmem_limit_bytes=24 * 1024 * 1024),
        name=name,
    )(*ins)


STEP = 1024


def projected(near_ref, far_ref, weight_ref, transposed):
    total = 0.0
    for at in range(0, near_ref.shape[-1], STEP):
        rows = [
            ref[:, :, at : at + STEP].astype(F32).reshape(HALF, STEP) for ref in (near_ref, far_ref)
        ]
        rows = jnp.concatenate(rows, axis=0).astype(BF)
        if transposed:
            total += dot_nt(rows, weight_ref[:, at : at + STEP])
        else:
            total += dot_nn(rows, weight_ref[at : at + STEP, :])
    return total


def mix(query_ref, keys, values, allowed, mixed_ref):
    for at in range(0, query_ref.shape[1], HD):
        _, probs = head_probs(query_ref[:, at : at + HD], keys, allowed)
        mixed_ref[:, at : at + HD] = dot_nn(probs.astype(BF), values).astype(BF)


def mix_back(query_ref, dmixed_ref, keys, values, allowed, dquery_ref, dkv_ref):
    dkeys = 0.0
    dvalues = 0.0
    for at in range(0, query_ref.shape[1], HD):
        query = query_ref[:, at : at + HD]
        query_cast, probs = head_probs(query, keys, allowed)
        dmixed = dmixed_ref[:, at : at + HD].astype(BF)
        dprobs = dot_nt(dmixed, values)
        dvalues += dot_tn(probs.astype(BF), dmixed)
        dscores = (
            probs * (dprobs - jnp.sum(probs * dprobs, axis=-1, keepdims=True)) * INV_SQRT
        ).astype(BF)
        dkeys += dot_tn(dscores, query_cast)
        dquery_ref[:, at : at + HD] = norm_back(query, dot_nn(dscores, keys), 1e-06).astype(BF)
    dkv_ref[:, :HD] = dkeys
    dkv_ref[:, HD:] = dvalues


def project(near, far, weight, transposed):
    def kernel(near_ref, far_ref, weight_ref, sum_ref):
        sum_ref[...] = projected(near_ref, far_ref, weight_ref, transposed)

    width = weight.shape[0] if transposed else weight.shape[1]
    return local_call(kernel, [((SEQ, width), F32)], [near, far, weight], "project")[0]


def attend(query, keys, values, allowed):
    def kernel(query_ref, keys_ref, values_ref, allowed_ref, mixed_ref):
        mix(query_ref, keys_ref[...], values_ref[...], allowed_ref[...], mixed_ref)

    return local_call(kernel, [(query.shape, BF)], [query, keys, values, allowed], "attend")[0]


def query_back(near, far, weight, dmixed, keys, values, allowed):
    def kernel(
        near_ref,
        far_ref,
        weight_ref,
        dmixed_ref,
        keys_ref,
        values_ref,
        allowed_ref,
        query_ref,
        dquery_ref,
        dkv_ref,
    ):
        query_ref[...] = projected(near_ref, far_ref, weight_ref, False)
        kv = (keys_ref[...], values_ref[...])
        mix_back(query_ref, dmixed_ref, *kv, allowed_ref[...], dquery_ref, dkv_ref)

    shape = (SEQ, weight.shape[1])
    return local_call(
        kernel,
        [(shape, F32), (shape, BF), ((VIS, 2 * HD), F32)],
        [near, far, weight, dmixed, keys, values, allowed],
        "query_back",
    )


def dmixed_back(near, far, weight, query, keys, values, allowed):
    def kernel(
        near_ref,
        far_ref,
        weight_ref,
        query_ref,
        keys_ref,
        values_ref,
        allowed_ref,
        dquery_ref,
        dkv_ref,
        dmixed_ref,
    ):
        dmixed_ref[...] = projected(near_ref, far_ref, weight_ref, True)
        kv = (keys_ref[...], values_ref[...])
        mix_back(query_ref, dmixed_ref, *kv, allowed_ref[...], dquery_ref, dkv_ref)

    return local_call(
        kernel,
        [(query.shape, BF), ((VIS, 2 * HD), F32)],
        [near, far, weight, query, keys, values, allowed],
        "dmixed_back",
        [pltpu.VMEM(query.shape, F32)],
    )


def weight_block(weight_ref, at, transposed):
    return weight_ref[at : at + STEP, :] if transposed else weight_ref[:, at : at + STEP]


def product(rows, weight, transposed):
    width = weight.shape[0] if transposed else weight.shape[1]

    def kernel(rows_ref, weight_ref, out_ref):
        dot = dot_nt if transposed else dot_nn
        for at in range(0, width, STEP):
            block = weight_block(weight_ref, at, transposed)
            out_ref[:, at : at + STEP] = dot(rows_ref[...], block).astype(BF)

    return local_call(kernel, [((HALF, width), BF)], [rows, weight], "product")[0]


def product_sum(rows, weight, arrived, transposed):
    width = arrived.shape[1]

    def kernel(rows_ref, weight_ref, arrived_ref, out_ref):
        dot = dot_nt if transposed else dot_nn
        for at in range(0, width, STEP):
            total = dot(rows_ref[...], weight_block(weight_ref, at, transposed))
            total += arrived_ref[:, at : at + STEP].astype(F32)
            out_ref[:, :, at : at + STEP] = total.reshape(CHIPS, ROWS, STEP).astype(BF)

    return local_call(
        kernel, [((CHIPS, ROWS, width), BF)], [rows, weight, arrived], "product_sum"
    )[0]


def chosen_product(first, rows, in_weight, out_weight):
    width = out_weight.shape[1]

    def kernel(first_ref, rows_ref, in_ref, out_weight_ref, out_ref):
        for transposed, ref in ((True, in_ref), (False, out_weight_ref)):

            @pl.when(first_ref[0] == int(transposed))
            def _():
                dot = dot_nt if transposed else dot_nn
                for at in range(0, width, STEP):
                    block = weight_block(ref, at, transposed)
                    out_ref[:, at : at + STEP] = dot(rows_ref[...], block).astype(BF)

    return chosen_call(
        kernel, ((HALF, width), BF), first, [rows, in_weight, out_weight], "chosen_product"
    )


def chosen_product_sum(first, rows, in_weight, out_weight, arrived):
    width = out_weight.shape[1]

    def kernel(first_ref, rows_ref, in_ref, out_weight_ref, arrived_ref, out_ref):
        for transposed, ref in ((True, in_ref), (False, out_weight_ref)):

            @pl.when(first_ref[0] == int(transposed))
            def _():
                dot = dot_nt if transposed else dot_nn
                for at in range(0, width, STEP):
                    total = dot(rows_ref[...], weight_block(ref, at, transposed))
                    total += arrived_ref[:, at : at + STEP].astype(F32)
                    out_ref[:, :, at : at + STEP] = total.reshape(CHIPS, ROWS, STEP).astype(BF)

    return chosen_call(
        kernel,
        ((CHIPS, ROWS, width), BF),
        first,
        [rows, in_weight, out_weight, arrived],
        "chosen_product_sum",
    )


def chosen_call(kernel, out, first, ins, name):
    held = pl.BlockSpec(memory_space=pltpu.VMEM)
    return pl.pallas_call(
        kernel,
        in_specs=[pl.BlockSpec(memory_space=pltpu.SMEM)] + [held] * len(ins),
        out_specs=held,
        out_shape=jax.ShapeDtypeStruct(*out),
        compiler_params=pltpu.CompilerParams(vmem_limit_bytes=24 * 1024 * 1024),
        name=name,
    )(first.astype(jnp.int32).reshape(1), *ins)


def token_sums(away_product, near_product, rows):
    away = away_product(rows[HALF:])
    return near_product(rows[:HALF], hop(away, TO_CORE))


def token_totals(terms):
    return jnp.sum(chip_exchange(terms).astype(F32), axis=0)


def kv_product(rows, w_key, w_value, arrived=None):
    def kernel(rows_ref, key_ref, value_ref, *refs):
        out_ref = refs[-1]
        for which, ref in enumerate((key_ref, value_ref)):
            part = dot_nn(rows_ref[...], ref[...])
            lanes = slice(which * HD, which * HD + HD)
            for chip in range(CHIPS):
                head, half = chip // 2, chip % 2
                piece = part[
                    half * TILE_ROWS : (half + 1) * TILE_ROWS, head * HD : (head + 1) * HD
                ]
                if arrived is not None:
                    piece = piece + refs[0][chip, :, lanes].astype(F32)
                out_ref[chip, :, lanes] = piece.astype(BF)

    more = [] if arrived is None else [arrived]
    return local_call(
        kernel,
        [((CHIPS, TILE_ROWS, 2 * HD), BF)],
        [rows, w_key, w_value, *more],
        "kv_product",
    )[0]


def vision_back(near, far, w_key, w_value):
    def kernel(near_ref, far_ref, key_ref, value_ref, out_ref):
        for core, ref in enumerate((near_ref, far_ref)):
            for half in range(2):
                total = 0.0
                for head in range(CHIPS // 2):
                    lanes = slice(head * HD, head * HD + HD)
                    piece = ref[2 * head + half]
                    total += dot_nt(piece[:, :HD], key_ref[:, lanes])
                    total += dot_nt(piece[:, HD:], value_ref[:, lanes])
                out_ref[half, core] = total

    return local_call(
        kernel,
        [((2, 2, TILE_ROWS, w_key.shape[0]), F32)],
        [near, far, w_key, w_value],
        "vision_back",
    )[0]


def weight_back(visions, near, far):
    samples = len(visions)
    heads = near.shape[0] // samples // 2

    def kernel(*refs):
        vision_refs = refs[:samples]
        near_ref, far_ref, key_ref, value_ref = refs[samples:]
        vision = jnp.concatenate([ref[...] for ref in vision_refs], axis=0)
        for head in range(heads):
            pieces = [
                ref[(sample * heads + head) * 2 + half]
                for sample in range(samples)
                for ref in (near_ref, far_ref)
                for half in range(2)
            ]
            total = dot_tn(vision, jnp.concatenate(pieces, axis=0))
            lanes = slice(head * HD, head * HD + HD)
            key_ref[:, lanes] = total[:, :HD]
            value_ref[:, lanes] = total[:, HD:]

    shape = ((visions[0].shape[-1], heads * HD), F32)
    return local_call(kernel, [shape, shape], [*visions, near, far], "weight_back")


def per_device(
    text,
    vision,
    query_weight,
    key_weight,
    value_weight,
    out_weight,
    gate,
    cotangent,
    tile_table,
    vision_tiles,
    text_lengths,
):
    section = lax.axis_index("depth")
    first = section == 0
    tensor = lax.axis_index("tensor")
    core = tensor % 2
    row = tensor // 16
    tile = tensor % 4
    w_key = key_weight[0]
    w_value = value_weight[0]
    gate_value = jnp.tanh(gate[0])
    depth_swap = [(0, 1), (1, 0)]
    text_f = text.astype(F32)
    cotangent_f = cotangent.astype(F32)

    opening = jnp.where(first, normalize(text_f, 1e-05), gate_value * cotangent_f).astype(BF)
    w_query = query_weight[0]
    w_out = out_weight[0]
    opened_near = chip_exchange(jnp.broadcast_to(opening[None], (CHIPS,) + opening.shape))

    place = jnp.arange(SEQ, dtype=jnp.int32)
    side = jnp.bitwise_xor(core, place // HALF)
    row_at = (place % HALF) // ROWS * (2 * ROWS) + side * ROWS + place % ROWS
    tile_ok = jnp.arange(TILES, dtype=jnp.int32) < vision_tiles[0]
    block_ok = ((tile_table[0] > 0) & tile_ok[None, :]).astype(BF)
    in_block = (row_at // TBLK)[:, None] == jnp.arange(SEQ // TBLK, dtype=jnp.int32)[None, :]
    in_block = in_block & (row_at < text_lengths[0])[:, None]
    column_tile = jnp.bitwise_xor(tile, jnp.arange(VIS, dtype=jnp.int32) // TILE_ROWS)
    in_tile = jnp.arange(TILES, dtype=jnp.int32)[:, None] == column_tile[None, :]
    allowed = dot_nn(dot_nn(in_block.astype(BF), block_ok).astype(BF), in_tile.astype(BF))

    other = lax.ppermute(vision, "depth", depth_swap)
    tiles = vision.reshape(2, TILE_ROWS, vision.shape[1])
    other_tiles = other.reshape(2, TILE_ROWS, vision.shape[1])

    def tiles_of(which):
        mine = jnp.where(which == 0, tiles[0], tiles[1])
        theirs = jnp.where(which == 0, other_tiles[0], other_tiles[1])
        return jnp.concatenate(
            [jnp.where(first, mine, theirs), jnp.where(first, theirs, mine)], axis=0
        )

    vision_near = tiles_of(core)
    vision_far = tiles_of(1 - core)
    vision_pair = jnp.concatenate([vision_near, vision_far], axis=0)
    samples = lax.axis_size("dp")

    def sample_hop(value, step):
        pairs = [(at, (at + step) % samples) for at in range(samples)]
        return lax.ppermute(value, "dp", pairs)

    vision_all = [vision_pair] + [sample_hop(vision_pair, step) for step in range(1, samples)]
    arrived = hop(kv_product(vision_far, w_key, w_value), TO_CORE)
    pieces = kv_product(vision_near, w_key, w_value, arrived)
    opened_near, pieces, vision_all = lax.optimization_barrier((opened_near, pieces, vision_all))
    opened = (opened_near, hop(opened_near, TO_CORE))
    query_first = project(*opened, w_query, False)
    pieces = after(chip_exchange(pieces), query_first)
    piece = jnp.sum(pieces.astype(F32), axis=0)
    keys_piece = piece[:, :HD]
    kv_piece = jnp.concatenate([normalize(keys_piece, 1e-06), piece[:, HD:]], axis=1).astype(BF)
    head_kv = jnp.concatenate(
        [kv_piece, hop(kv_piece, TO_CORE), hop(kv_piece, KV_PAIR), hop(kv_piece, KV_BOTH)], axis=0
    )
    keys = head_kv[:, :HD]
    values = head_kv[:, HD:]

    def out_sums(rows):
        return token_sums(
            lambda part: product(part, w_out, False),
            lambda part, arrived: product_sum(part, w_out, arrived, False),
            rows,
        )

    def in_sums(rows):
        return token_sums(
            lambda part: product(part, w_query, True),
            lambda part, arrived: product_sum(part, w_query, arrived, True),
            rows,
        )

    def last_sums(rows):
        return token_sums(
            lambda part: chosen_product(first, part, w_query, w_out),
            lambda part, arrived: chosen_product_sum(first, part, w_query, w_out, arrived),
            rows,
        )

    dmixed_second = project(*opened, w_out, True)
    mixed_first = attend(query_first, keys, values, allowed)
    hidden_first = (text_f + gate_value * token_totals(out_sums(mixed_first))).astype(BF)

    passed = lax.ppermute(hidden_first, "depth", [(0, 1)])
    passed_f = passed.astype(F32)
    middle = gather_chips(normalize(passed_f, 1e-05).astype(BF))
    query_second, dquery_second, dkv_second = query_back(
        *middle, w_query, dmixed_second, keys, values, allowed
    )
    dnormed = token_totals(in_sums(dquery_second))
    grad_second = (cotangent_f + norm_back(passed_f, dnormed, 1e-05)).astype(BF)
    mixed_second = attend(query_second, keys, values, allowed)

    upstream = lax.ppermute(grad_second, "depth", [(1, 0)])
    upstream_f = upstream.astype(F32)
    closing = gather_chips((gate_value * upstream_f).astype(BF))
    dquery_first, dkv_first = dmixed_back(*closing, w_out, query_first, keys, values, allowed)

    dkv = jnp.where(first, dkv_first, dkv_second)
    dkv_piece = (
        dkv[:TILE_ROWS]
        + hop(dkv[TILE_ROWS : 2 * TILE_ROWS], TO_CORE)
        + hop(dkv[2 * TILE_ROWS : 3 * TILE_ROWS], KV_PAIR)
        + hop(dkv[3 * TILE_ROWS :], KV_BOTH)
    )
    dkv_piece = jnp.concatenate(
        [norm_back(keys_piece, dkv_piece[:, :HD], 1e-06), dkv_piece[:, HD:]], axis=1
    ).astype(BF)
    ring_pieces = ring_exchange(jnp.broadcast_to(dkv_piece[None], (RING,) + dkv_piece.shape))
    last_terms = last_sums(jnp.where(first, dquery_first, mixed_second))
    ring_pieces, last_terms = lax.optimization_barrier((ring_pieces, last_terms))
    other_pieces = hop(ring_pieces, TO_ROW)
    pieces_near = jnp.concatenate(
        [
            jnp.where(row == 0, ring_pieces, other_pieces),
            jnp.where(row == 0, other_pieces, ring_pieces),
        ],
        axis=0,
    )
    pieces_far = hop(pieces_near, TO_CORE)
    sample = lax.axis_index("dp")
    share = CHIPS // samples
    columns = []
    for step in range(samples):
        start = (sample + step) % samples * share
        column = lax.dynamic_slice_in_dim(pieces_near, start, share, 0)
        columns.append(sample_hop(column, step) if step else column)
    columns_near = jnp.concatenate(columns, axis=0)
    columns_far = hop(columns_near, TO_CORE)
    key_grad, value_grad = weight_back(vision_all, columns_near, columns_far)
    dvision = vision_back(pieces_near, pieces_far, w_key, w_value)
    mine = lax.dynamic_index_in_dim(dvision, section, 0, False)
    theirs = lax.dynamic_index_in_dim(dvision, 1 - section, 0, False)
    dvision = mine + lax.ppermute(theirs, "depth", depth_swap)
    dvision = jnp.where(core == 0, dvision, dvision[::-1]).reshape(VIS // 2, vision.shape[1])

    last = token_totals(last_terms)
    grad_first = (upstream_f + norm_back(text_f, last, 1e-05)).astype(BF)
    hidden_second = (passed_f + gate_value * last).astype(BF)
    hidden = jnp.where(first, hidden_first, hidden_second)
    text_grad = jnp.where(first, grad_first, grad_second)
    return (hidden[None], text_grad[None], dvision, key_grad[None], value_grad[None])


def solution(mesh):
    in_specs = (
        P(("dp", "tensor"), None),
        P(("dp", "depth"), "tensor"),
        P("depth", None, "tensor"),
        P("depth", "tensor", None),
        P("depth", "tensor", None),
        P("depth", "tensor", None),
        P("depth"),
        P(("dp", "tensor"), None),
        P("dp", None, None),
        P("dp"),
        P("dp"),
    )
    out_specs = (
        P("depth", ("dp", "tensor"), None),
        P("depth", ("dp", "tensor"), None),
        P(("dp", "depth"), "tensor"),
        P("depth", "tensor", "dp"),
        P("depth", "tensor", "dp"),
    )
    return jax.shard_map(
        per_device, mesh=mesh, in_specs=in_specs, out_specs=out_specs, check_vma=False
    )
```

```python
import math

import jax
import jax.numpy as jnp
from jax import lax
from jax.experimental import pallas as pl
from jax.experimental.pallas import tpu as pltpu
from jax.sharding import PartitionSpec as P

HD = 128
SEQ = 128
TBLK = 16
TILES = 4
TILE_ROWS = 64
VIS = 256
NT = 32
INV_SQRT = 1.0 / math.sqrt(HD)
BF = jnp.bfloat16
F32 = jnp.float32


def moved(move):
    pairs = []
    for t in range(NT):
        y, z, c = move(t // 16, (t // 2) % 8, t % 2)
        pairs.append((t, y * 16 + z * 2 + c))
    return pairs


TO_CORE = moved(lambda y, z, c: (y, z, 1 - c))
TO_ROW = moved(lambda y, z, c: (1 - y, z, c))
KV_PAIR = moved(lambda y, z, c: (y, z ^ 1, c))
KV_BOTH = moved(lambda y, z, c: (y, z ^ 1, 1 - c))
CHIPS = NT // 2
CHIP_GROUPS = [[2 * chip + c for chip in range(CHIPS)] for c in range(2)]
RING = 8
RING_GROUPS = [[16 * y + 2 * z + c for z in range(RING)] for y in range(2) for c in range(2)]
ROWS = SEQ // NT
HALF = SEQ // 2


def hop(value, pairs):
    return lax.ppermute(value, "tensor", pairs)


def chip_exchange(value):
    return lax.all_to_all(value, "tensor", 0, 0, axis_index_groups=CHIP_GROUPS)


def ring_exchange(value):
    return lax.all_to_all(value, "tensor", 0, 0, axis_index_groups=RING_GROUPS)


def after(value, earlier):
    return lax.optimization_barrier((value, earlier))[0]


def gather_chips(shard):
    near = chip_exchange(jnp.broadcast_to(shard[None], (CHIPS,) + shard.shape))
    return near, hop(near, TO_CORE)


def normalize(values, epsilon):
    return values * lax.rsqrt(jnp.mean(values * values, axis=-1, keepdims=True) + epsilon)


def norm_back(values, upstream, epsilon):
    inv_rms = lax.rsqrt(jnp.mean(values * values, axis=-1, keepdims=True) + epsilon)
    normed = values * inv_rms
    return inv_rms * (upstream - normed * jnp.mean(upstream * normed, axis=-1, keepdims=True))


def dot_nt(a, b):
    return lax.dot_general(a, b, (((1,), (1,)), ((), ())), preferred_element_type=F32)


def dot_tn(a, b):
    return lax.dot_general(a, b, (((0,), (0,)), ((), ())), preferred_element_type=F32)


def dot_nn(a, b):
    return lax.dot_general(a, b, (((1,), (0,)), ((), ())), preferred_element_type=F32)


def head_probs(query, keys, allowed):
    query_cast = normalize(query, 1e-06).astype(BF)
    scores = dot_nt(query_cast, keys) * INV_SQRT
    expd = jnp.where(allowed > 0.0, jnp.exp(scores), 0.0)
    live = jnp.max(allowed, axis=-1, keepdims=True)
    probs = expd / (jnp.sum(expd, axis=-1, keepdims=True) + (1.0 - live))
    return query_cast, probs


def local_call(kernel, outs, ins, name, scratch=()):
    held = pl.BlockSpec(memory_space=pltpu.VMEM)
    return pl.pallas_call(
        kernel,
        in_specs=[held] * len(ins),
        out_specs=[held] * len(outs),
        out_shape=[jax.ShapeDtypeStruct(shape, dtype) for shape, dtype in outs],
        scratch_shapes=list(scratch),
        compiler_params=pltpu.CompilerParams(vmem_limit_bytes=24 * 1024 * 1024),
        name=name,
    )(*ins)


STEP = 1024


def projected(near_ref, far_ref, weight_ref, transposed):
    total = 0.0
    for at in range(0, near_ref.shape[-1], STEP):
        rows = [
            ref[:, :, at : at + STEP].astype(F32).reshape(HALF, STEP) for ref in (near_ref, far_ref)
        ]
        rows = jnp.concatenate(rows, axis=0).astype(BF)
        if transposed:
            total += dot_nt(rows, weight_ref[:, at : at + STEP])
        else:
            total += dot_nn(rows, weight_ref[at : at + STEP, :])
    return total


def mix(query_ref, keys, values, allowed, mixed_ref):
    for at in range(0, query_ref.shape[1], HD):
        _, probs = head_probs(query_ref[:, at : at + HD], keys, allowed)
        mixed_ref[:, at : at + HD] = dot_nn(probs.astype(BF), values).astype(BF)


def mix_back(query_ref, dmixed_ref, keys, values, allowed, dquery_ref, dkv_ref):
    dkeys = 0.0
    dvalues = 0.0
    for at in range(0, query_ref.shape[1], HD):
        query = query_ref[:, at : at + HD]
        query_cast, probs = head_probs(query, keys, allowed)
        dmixed = dmixed_ref[:, at : at + HD].astype(BF)
        dprobs = dot_nt(dmixed, values)
        dvalues += dot_tn(probs.astype(BF), dmixed)
        dscores = (
            probs * (dprobs - jnp.sum(probs * dprobs, axis=-1, keepdims=True)) * INV_SQRT
        ).astype(BF)
        dkeys += dot_tn(dscores, query_cast)
        dquery_ref[:, at : at + HD] = norm_back(query, dot_nn(dscores, keys), 1e-06).astype(BF)
    dkv_ref[:, :HD] = dkeys
    dkv_ref[:, HD:] = dvalues


def project(near, far, weight, transposed):
    def kernel(near_ref, far_ref, weight_ref, sum_ref):
        sum_ref[...] = projected(near_ref, far_ref, weight_ref, transposed)

    width = weight.shape[0] if transposed else weight.shape[1]
    return local_call(kernel, [((SEQ, width), F32)], [near, far, weight], "project")[0]


def attend(query, keys, values, allowed):
    def kernel(query_ref, keys_ref, values_ref, allowed_ref, mixed_ref):
        mix(query_ref, keys_ref[...], values_ref[...], allowed_ref[...], mixed_ref)

    return local_call(kernel, [(query.shape, BF)], [query, keys, values, allowed], "attend")[0]


def query_back(near, far, weight, dmixed, keys, values, allowed):
    def kernel(
        near_ref,
        far_ref,
        weight_ref,
        dmixed_ref,
        keys_ref,
        values_ref,
        allowed_ref,
        query_ref,
        dquery_ref,
        dkv_ref,
    ):
        query_ref[...] = projected(near_ref, far_ref, weight_ref, False)
        kv = (keys_ref[...], values_ref[...])
        mix_back(query_ref, dmixed_ref, *kv, allowed_ref[...], dquery_ref, dkv_ref)

    shape = (SEQ, weight.shape[1])
    return local_call(
        kernel,
        [(shape, F32), (shape, BF), ((VIS, 2 * HD), F32)],
        [near, far, weight, dmixed, keys, values, allowed],
        "query_back",
    )


def dmixed_back(near, far, weight, query, keys, values, allowed):
    def kernel(
        near_ref,
        far_ref,
        weight_ref,
        query_ref,
        keys_ref,
        values_ref,
        allowed_ref,
        dquery_ref,
        dkv_ref,
        dmixed_ref,
    ):
        dmixed_ref[...] = projected(near_ref, far_ref, weight_ref, True)
        kv = (keys_ref[...], values_ref[...])
        mix_back(query_ref, dmixed_ref, *kv, allowed_ref[...], dquery_ref, dkv_ref)

    return local_call(
        kernel,
        [(query.shape, BF), ((VIS, 2 * HD), F32)],
        [near, far, weight, query, keys, values, allowed],
        "dmixed_back",
        [pltpu.VMEM(query.shape, F32)],
    )


def weight_block(weight_ref, at, transposed):
    return weight_ref[at : at + STEP, :] if transposed else weight_ref[:, at : at + STEP]


def product(rows, weight, transposed):
    width = weight.shape[0] if transposed else weight.shape[1]

    def kernel(rows_ref, weight_ref, out_ref):
        dot = dot_nt if transposed else dot_nn
        for at in range(0, width, STEP):
            block = weight_block(weight_ref, at, transposed)
            out_ref[:, at : at + STEP] = dot(rows_ref[...], block).astype(BF)

    return local_call(kernel, [((HALF, width), BF)], [rows, weight], "product")[0]


def product_sum(rows, weight, arrived, transposed):
    width = arrived.shape[1]

    def kernel(rows_ref, weight_ref, arrived_ref, out_ref):
        dot = dot_nt if transposed else dot_nn
        for at in range(0, width, STEP):
            total = dot(rows_ref[...], weight_block(weight_ref, at, transposed))
            total += arrived_ref[:, at : at + STEP].astype(F32)
            out_ref[:, :, at : at + STEP] = total.reshape(CHIPS, ROWS, STEP).astype(BF)

    return local_call(
        kernel, [((CHIPS, ROWS, width), BF)], [rows, weight, arrived], "product_sum"
    )[0]


def chosen_product(first, rows, in_weight, out_weight):
    width = out_weight.shape[1]

    def kernel(first_ref, rows_ref, in_ref, out_weight_ref, out_ref):
        for transposed, ref in ((True, in_ref), (False, out_weight_ref)):

            @pl.when(first_ref[0] == int(transposed))
            def _():
                dot = dot_nt if transposed else dot_nn
                for at in range(0, width, STEP):
                    block = weight_block(ref, at, transposed)
                    out_ref[:, at : at + STEP] = dot(rows_ref[...], block).astype(BF)

    return chosen_call(
        kernel, ((HALF, width), BF), first, [rows, in_weight, out_weight], "chosen_product"
    )


def chosen_product_sum(first, rows, in_weight, out_weight, arrived):
    width = out_weight.shape[1]

    def kernel(first_ref, rows_ref, in_ref, out_weight_ref, arrived_ref, out_ref):
        for transposed, ref in ((True, in_ref), (False, out_weight_ref)):

            @pl.when(first_ref[0] == int(transposed))
            def _():
                dot = dot_nt if transposed else dot_nn
                for at in range(0, width, STEP):
                    total = dot(rows_ref[...], weight_block(ref, at, transposed))
                    total += arrived_ref[:, at : at + STEP].astype(F32)
                    out_ref[:, :, at : at + STEP] = total.reshape(CHIPS, ROWS, STEP).astype(BF)

    return chosen_call(
        kernel,
        ((CHIPS, ROWS, width), BF),
        first,
        [rows, in_weight, out_weight, arrived],
        "chosen_product_sum",
    )


def chosen_call(kernel, out, first, ins, name):
    held = pl.BlockSpec(memory_space=pltpu.VMEM)
    return pl.pallas_call(
        kernel,
        in_specs=[pl.BlockSpec(memory_space=pltpu.SMEM)] + [held] * len(ins),
        out_specs=held,
        out_shape=jax.ShapeDtypeStruct(*out),
        compiler_params=pltpu.CompilerParams(vmem_limit_bytes=24 * 1024 * 1024),
        name=name,
    )(first.astype(jnp.int32).reshape(1), *ins)


def chips_sum(pieces_ref):
    total = pieces_ref[0].astype(F32)
    for chip in range(1, CHIPS):
        total += pieces_ref[chip].astype(F32)
    return total


def input_grad(upstream_ref, inputs_ref, total):
    back = norm_back(inputs_ref[...].astype(F32), total, 1e-05)
    return (upstream_ref[...].astype(F32) + back).astype(BF)


def grad_rows(pieces, upstream, inputs):
    def kernel(pieces_ref, upstream_ref, inputs_ref, grad_ref):
        grad_ref[...] = input_grad(upstream_ref, inputs_ref, chips_sum(pieces_ref))

    return local_call(kernel, [(inputs.shape, BF)], [pieces, upstream, inputs], "grad_rows")[0]


def last_rows(first, gate_value, pieces, text, upstream, hidden, passed, grad):
    def kernel(
        first_ref,
        gate_ref,
        pieces_ref,
        text_ref,
        upstream_ref,
        hidden_ref,
        passed_ref,
        grad_ref,
        hidden_out_ref,
        grad_out_ref,
    ):
        total = chips_sum(pieces_ref)

        @pl.when(first_ref[0] == 1)
        def _():
            hidden_out_ref[...] = hidden_ref[...]
            grad_out_ref[...] = input_grad(upstream_ref, text_ref, total)

        @pl.when(first_ref[0] == 0)
        def _():
            term = gate_ref[0] * total
            hidden_out_ref[...] = (passed_ref[...].astype(F32) + term).astype(BF)
            grad_out_ref[...] = grad_ref[...]

    scalar = pl.BlockSpec(memory_space=pltpu.SMEM)
    shape = jax.ShapeDtypeStruct(text.shape, BF)
    return pl.pallas_call(
        kernel,
        in_specs=[scalar, scalar] + [pl.BlockSpec()] * 6,
        out_shape=[shape, shape],
        compiler_params=pltpu.CompilerParams(vmem_limit_bytes=24 * 1024 * 1024),
        name="last_rows",
    )(
        first.astype(jnp.int32).reshape(1),
        gate_value.reshape(1),
        pieces,
        text,
        upstream,
        hidden,
        passed,
        grad,
    )


def token_sums(away_product, near_product, rows):
    away = away_product(rows[HALF:])
    return near_product(rows[:HALF], hop(away, TO_CORE))


def kv_product(rows, w_key, w_value, arrived=None):
    def kernel(rows_ref, key_ref, value_ref, *refs):
        out_ref = refs[-1]
        for which, ref in enumerate((key_ref, value_ref)):
            part = dot_nn(rows_ref[...], ref[...])
            lanes = slice(which * HD, which * HD + HD)
            for chip in range(CHIPS):
                head, half = chip // 2, chip % 2
                piece = part[
                    half * TILE_ROWS : (half + 1) * TILE_ROWS, head * HD : (head + 1) * HD
                ]
                if arrived is not None:
                    piece = piece + refs[0][chip, :, lanes].astype(F32)
                out_ref[chip, :, lanes] = piece.astype(BF)

    more = [] if arrived is None else [arrived]
    return local_call(
        kernel,
        [((CHIPS, TILE_ROWS, 2 * HD), BF)],
        [rows, w_key, w_value, *more],
        "kv_product",
    )[0]


def vision_back(near, far, w_key, w_value):
    def kernel(near_ref, far_ref, key_ref, value_ref, out_ref):
        for core, ref in enumerate((near_ref, far_ref)):
            for half in range(2):
                total = 0.0
                for head in range(CHIPS // 2):
                    lanes = slice(head * HD, head * HD + HD)
                    piece = ref[2 * head + half]
                    total += dot_nt(piece[:, :HD], key_ref[:, lanes])
                    total += dot_nt(piece[:, HD:], value_ref[:, lanes])
                out_ref[half, core] = total

    return local_call(
        kernel,
        [((2, 2, TILE_ROWS, w_key.shape[0]), F32)],
        [near, far, w_key, w_value],
        "vision_back",
    )[0]


def weight_back(visions, near, far):
    samples = len(visions)
    heads = near.shape[0] // samples // 2

    def kernel(*refs):
        vision_refs = refs[:samples]
        near_ref, far_ref, key_ref, value_ref = refs[samples:]
        vision = jnp.concatenate([ref[...] for ref in vision_refs], axis=0)
        for head in range(heads):
            pieces = [
                ref[(sample * heads + head) * 2 + half]
                for sample in range(samples)
                for ref in (near_ref, far_ref)
                for half in range(2)
            ]
            total = dot_tn(vision, jnp.concatenate(pieces, axis=0))
            lanes = slice(head * HD, head * HD + HD)
            key_ref[:, lanes] = total[:, :HD]
            value_ref[:, lanes] = total[:, HD:]

    shape = ((visions[0].shape[-1], heads * HD), F32)
    return local_call(kernel, [shape, shape], [*visions, near, far], "weight_back")


def per_device(
    text,
    vision,
    query_weight,
    key_weight,
    value_weight,
    out_weight,
    gate,
    cotangent,
    tile_table,
    vision_tiles,
    text_lengths,
):
    section = lax.axis_index("depth")
    first = section == 0
    tensor = lax.axis_index("tensor")
    core = tensor % 2
    row = tensor // 16
    tile = tensor % 4
    w_key = key_weight[0]
    w_value = value_weight[0]
    gate_value = jnp.tanh(gate[0])
    depth_swap = [(0, 1), (1, 0)]
    text_f = text.astype(F32)
    cotangent_f = cotangent.astype(F32)

    opening = jnp.where(first, normalize(text_f, 1e-05), gate_value * cotangent_f).astype(BF)
    w_query = query_weight[0]
    w_out = out_weight[0]
    opened_near = chip_exchange(jnp.broadcast_to(opening[None], (CHIPS,) + opening.shape))

    place = jnp.arange(SEQ, dtype=jnp.int32)
    side = jnp.bitwise_xor(core, place // HALF)
    row_at = (place % HALF) // ROWS * (2 * ROWS) + side * ROWS + place % ROWS
    tile_ok = jnp.arange(TILES, dtype=jnp.int32) < vision_tiles[0]
    block_ok = ((tile_table[0] > 0) & tile_ok[None, :]).astype(BF)
    in_block = (row_at // TBLK)[:, None] == jnp.arange(SEQ // TBLK, dtype=jnp.int32)[None, :]
    in_block = in_block & (row_at < text_lengths[0])[:, None]
    column_tile = jnp.bitwise_xor(tile, jnp.arange(VIS, dtype=jnp.int32) // TILE_ROWS)
    in_tile = jnp.arange(TILES, dtype=jnp.int32)[:, None] == column_tile[None, :]
    allowed = dot_nn(dot_nn(in_block.astype(BF), block_ok).astype(BF), in_tile.astype(BF))

    other = lax.ppermute(vision, "depth", depth_swap)
    tiles = vision.reshape(2, TILE_ROWS, vision.shape[1])
    other_tiles = other.reshape(2, TILE_ROWS, vision.shape[1])

    def tiles_of(which):
        mine = jnp.where(which == 0, tiles[0], tiles[1])
        theirs = jnp.where(which == 0, other_tiles[0], other_tiles[1])
        return jnp.concatenate(
            [jnp.where(first, mine, theirs), jnp.where(first, theirs, mine)], axis=0
        )

    vision_near = tiles_of(core)
    vision_far = tiles_of(1 - core)
    vision_pair = jnp.concatenate([vision_near, vision_far], axis=0)
    samples = lax.axis_size("dp")

    def sample_hop(value, step):
        pairs = [(at, (at + step) % samples) for at in range(samples)]
        return lax.ppermute(value, "dp", pairs)

    vision_all = [vision_pair] + [sample_hop(vision_pair, step) for step in range(1, samples)]
    arrived = hop(kv_product(vision_far, w_key, w_value), TO_CORE)
    pieces = kv_product(vision_near, w_key, w_value, arrived)
    opened_near, pieces, vision_all = lax.optimization_barrier((opened_near, pieces, vision_all))
    opened = (opened_near, hop(opened_near, TO_CORE))
    query_first = project(*opened, w_query, False)
    pieces = after(chip_exchange(pieces), query_first)
    piece = jnp.sum(pieces.astype(F32), axis=0)
    keys_piece = piece[:, :HD]
    kv_piece = jnp.concatenate([normalize(keys_piece, 1e-06), piece[:, HD:]], axis=1).astype(BF)
    head_kv = jnp.concatenate(
        [kv_piece, hop(kv_piece, TO_CORE), hop(kv_piece, KV_PAIR), hop(kv_piece, KV_BOTH)], axis=0
    )
    keys = head_kv[:, :HD]
    values = head_kv[:, HD:]

    def out_sums(rows):
        return token_sums(
            lambda part: product(part, w_out, False),
            lambda part, arrived: product_sum(part, w_out, arrived, False),
            rows,
        )

    def in_sums(rows):
        return token_sums(
            lambda part: product(part, w_query, True),
            lambda part, arrived: product_sum(part, w_query, arrived, True),
            rows,
        )

    def last_sums(rows):
        return token_sums(
            lambda part: chosen_product(first, part, w_query, w_out),
            lambda part, arrived: chosen_product_sum(first, part, w_query, w_out, arrived),
            rows,
        )

    dmixed_second = project(*opened, w_out, True)
    mixed_first = attend(query_first, keys, values, allowed)
    attended = jnp.sum(chip_exchange(out_sums(mixed_first)).astype(F32), axis=0)
    hidden_first = (text_f + gate_value * attended).astype(BF)

    passed = lax.ppermute(hidden_first, "depth", [(0, 1)])
    passed_f = passed.astype(F32)
    middle = gather_chips(normalize(passed_f, 1e-05).astype(BF))
    query_second, dquery_second, dkv_second = query_back(
        *middle, w_query, dmixed_second, keys, values, allowed
    )
    grad_second = grad_rows(chip_exchange(in_sums(dquery_second)), cotangent, passed)
    mixed_second = attend(query_second, keys, values, allowed)

    upstream = lax.ppermute(grad_second, "depth", [(1, 0)])
    upstream_f = upstream.astype(F32)
    closing = gather_chips((gate_value * upstream_f).astype(BF))
    dquery_first, dkv_first = dmixed_back(*closing, w_out, query_first, keys, values, allowed)

    dkv = jnp.where(first, dkv_first, dkv_second)
    dkv_piece = (
        dkv[:TILE_ROWS]
        + hop(dkv[TILE_ROWS : 2 * TILE_ROWS], TO_CORE)
        + hop(dkv[2 * TILE_ROWS : 3 * TILE_ROWS], KV_PAIR)
        + hop(dkv[3 * TILE_ROWS :], KV_BOTH)
    )
    dkv_piece = jnp.concatenate(
        [norm_back(keys_piece, dkv_piece[:, :HD], 1e-06), dkv_piece[:, HD:]], axis=1
    ).astype(BF)
    ring_pieces = ring_exchange(jnp.broadcast_to(dkv_piece[None], (RING,) + dkv_piece.shape))
    last_terms = last_sums(jnp.where(first, dquery_first, mixed_second))
    ring_pieces, last_terms = lax.optimization_barrier((ring_pieces, last_terms))
    other_pieces = hop(ring_pieces, TO_ROW)
    pieces_near = jnp.concatenate(
        [
            jnp.where(row == 0, ring_pieces, other_pieces),
            jnp.where(row == 0, other_pieces, ring_pieces),
        ],
        axis=0,
    )
    pieces_far = hop(pieces_near, TO_CORE)
    sample = lax.axis_index("dp")
    share = CHIPS // samples
    columns = []
    for step in range(samples):
        start = (sample + step) % samples * share
        column = lax.dynamic_slice_in_dim(pieces_near, start, share, 0)
        columns.append(sample_hop(column, step) if step else column)
    columns_near = jnp.concatenate(columns, axis=0)
    columns_far = hop(columns_near, TO_CORE)
    key_grad, value_grad = weight_back(vision_all, columns_near, columns_far)
    dvision = vision_back(pieces_near, pieces_far, w_key, w_value)
    mine = lax.dynamic_index_in_dim(dvision, section, 0, False)
    theirs = lax.dynamic_index_in_dim(dvision, 1 - section, 0, False)
    dvision = mine + lax.ppermute(theirs, "depth", depth_swap)
    dvision = jnp.where(core == 0, dvision, dvision[::-1]).reshape(VIS // 2, vision.shape[1])

    hidden, text_grad = last_rows(
        first,
        gate_value,
        chip_exchange(last_terms),
        text,
        upstream,
        hidden_first,
        passed,
        grad_second,
    )
    return (hidden[None], text_grad[None], dvision, key_grad[None], value_grad[None])


def solution(mesh):
    in_specs = (
        P(("dp", "tensor"), None),
        P(("dp", "depth"), "tensor"),
        P("depth", None, "tensor"),
        P("depth", "tensor", None),
        P("depth", "tensor", None),
        P("depth", "tensor", None),
        P("depth"),
        P(("dp", "tensor"), None),
        P("dp", None, None),
        P("dp"),
        P("dp"),
    )
    out_specs = (
        P("depth", ("dp", "tensor"), None),
        P("depth", ("dp", "tensor"), None),
        P(("dp", "depth"), "tensor"),
        P("depth", "tensor", "dp"),
        P("depth", "tensor", "dp"),
    )
    return jax.shard_map(
        per_device, mesh=mesh, in_specs=in_specs, out_specs=out_specs, check_vma=False
    )
```

```python
import math

import jax
import jax.numpy as jnp
from jax import lax
from jax.experimental import pallas as pl
from jax.experimental.pallas import tpu as pltpu
from jax.sharding import PartitionSpec as P

HD = 128
SEQ = 128
TBLK = 16
TILES = 4
TILE_ROWS = 64
VIS = 256
NT = 32
INV_SQRT = 1.0 / math.sqrt(HD)
BF = jnp.bfloat16
F32 = jnp.float32


def moved(move):
    pairs = []
    for t in range(NT):
        y, z, c = move(t // 16, (t // 2) % 8, t % 2)
        pairs.append((t, y * 16 + z * 2 + c))
    return pairs


TO_CORE = moved(lambda y, z, c: (y, z, 1 - c))
TO_ROW = moved(lambda y, z, c: (1 - y, z, c))
KV_PAIR = moved(lambda y, z, c: (y, z ^ 1, c))
KV_BOTH = moved(lambda y, z, c: (y, z ^ 1, 1 - c))
CHIPS = NT // 2
CHIP_GROUPS = [[2 * chip + c for chip in range(CHIPS)] for c in range(2)]
RING = 8
RING_GROUPS = [[16 * y + 2 * z + c for z in range(RING)] for y in range(2) for c in range(2)]
ROWS = SEQ // NT
HALF = SEQ // 2


def hop(value, pairs):
    return lax.ppermute(value, "tensor", pairs)


def chip_exchange(value):
    return lax.all_to_all(value, "tensor", 0, 0, axis_index_groups=CHIP_GROUPS)


def ring_exchange(value):
    return lax.all_to_all(value, "tensor", 0, 0, axis_index_groups=RING_GROUPS)


def after(value, earlier):
    return lax.optimization_barrier((value, earlier))[0]


def gather_chips(shard):
    near = chip_exchange(jnp.broadcast_to(shard[None], (CHIPS,) + shard.shape))
    return near, hop(near, TO_CORE)


def normalize(values, epsilon):
    return values * lax.rsqrt(jnp.mean(values * values, axis=-1, keepdims=True) + epsilon)


def norm_back(values, upstream, epsilon):
    inv_rms = lax.rsqrt(jnp.mean(values * values, axis=-1, keepdims=True) + epsilon)
    normed = values * inv_rms
    return inv_rms * (upstream - normed * jnp.mean(upstream * normed, axis=-1, keepdims=True))


def dot_nt(a, b):
    return lax.dot_general(a, b, (((1,), (1,)), ((), ())), preferred_element_type=F32)


def dot_tn(a, b):
    return lax.dot_general(a, b, (((0,), (0,)), ((), ())), preferred_element_type=F32)


def dot_nn(a, b):
    return lax.dot_general(a, b, (((1,), (0,)), ((), ())), preferred_element_type=F32)


def head_probs(query, keys, allowed):
    query_cast = normalize(query, 1e-06).astype(BF)
    scores = dot_nt(query_cast, keys) * INV_SQRT
    expd = jnp.where(allowed > 0.0, jnp.exp(scores), 0.0)
    live = jnp.max(allowed, axis=-1, keepdims=True)
    probs = expd / (jnp.sum(expd, axis=-1, keepdims=True) + (1.0 - live))
    return query_cast, probs


def local_call(kernel, outs, ins, name, scratch=()):
    held = pl.BlockSpec(memory_space=pltpu.VMEM)
    return pl.pallas_call(
        kernel,
        in_specs=[held] * len(ins),
        out_specs=[held] * len(outs),
        out_shape=[jax.ShapeDtypeStruct(shape, dtype) for shape, dtype in outs],
        scratch_shapes=list(scratch),
        compiler_params=pltpu.CompilerParams(vmem_limit_bytes=24 * 1024 * 1024),
        name=name,
    )(*ins)


STEP = 1024


def projected(near_ref, far_ref, weight_ref, transposed):
    total = 0.0
    for at in range(0, near_ref.shape[-1], STEP):
        rows = [
            ref[:, :, at : at + STEP].astype(F32).reshape(HALF, STEP) for ref in (near_ref, far_ref)
        ]
        rows = jnp.concatenate(rows, axis=0).astype(BF)
        if transposed:
            total += dot_nt(rows, weight_ref[:, at : at + STEP])
        else:
            total += dot_nn(rows, weight_ref[at : at + STEP, :])
    return total


def mix(query_ref, keys, values, allowed, mixed_ref):
    for at in range(0, query_ref.shape[1], HD):
        _, probs = head_probs(query_ref[:, at : at + HD], keys, allowed)
        mixed_ref[:, at : at + HD] = dot_nn(probs.astype(BF), values).astype(BF)


def mix_back(query_ref, dmixed_ref, keys, values, allowed, dquery_ref, dkv_ref):
    dkeys = 0.0
    dvalues = 0.0
    for at in range(0, query_ref.shape[1], HD):
        query = query_ref[:, at : at + HD]
        query_cast, probs = head_probs(query, keys, allowed)
        dmixed = dmixed_ref[:, at : at + HD].astype(BF)
        dprobs = dot_nt(dmixed, values)
        dvalues += dot_tn(probs.astype(BF), dmixed)
        dscores = (
            probs * (dprobs - jnp.sum(probs * dprobs, axis=-1, keepdims=True)) * INV_SQRT
        ).astype(BF)
        dkeys += dot_tn(dscores, query_cast)
        dquery_ref[:, at : at + HD] = norm_back(query, dot_nn(dscores, keys), 1e-06).astype(BF)
    dkv_ref[:, :HD] = dkeys
    dkv_ref[:, HD:] = dvalues


def project(near, far, weight, transposed):
    def kernel(near_ref, far_ref, weight_ref, sum_ref):
        sum_ref[...] = projected(near_ref, far_ref, weight_ref, transposed)

    width = weight.shape[0] if transposed else weight.shape[1]
    return local_call(kernel, [((SEQ, width), F32)], [near, far, weight], "project")[0]


def attend(query, keys, values, allowed):
    def kernel(query_ref, keys_ref, values_ref, allowed_ref, mixed_ref):
        mix(query_ref, keys_ref[...], values_ref[...], allowed_ref[...], mixed_ref)

    return local_call(kernel, [(query.shape, BF)], [query, keys, values, allowed], "attend")[0]


def query_back(near, far, weight, dmixed, keys, values, allowed):
    def kernel(
        near_ref,
        far_ref,
        weight_ref,
        dmixed_ref,
        keys_ref,
        values_ref,
        allowed_ref,
        query_ref,
        dquery_ref,
        dkv_ref,
    ):
        query_ref[...] = projected(near_ref, far_ref, weight_ref, False)
        kv = (keys_ref[...], values_ref[...])
        mix_back(query_ref, dmixed_ref, *kv, allowed_ref[...], dquery_ref, dkv_ref)

    shape = (SEQ, weight.shape[1])
    return local_call(
        kernel,
        [(shape, F32), (shape, BF), ((VIS, 2 * HD), F32)],
        [near, far, weight, dmixed, keys, values, allowed],
        "query_back",
    )


def dmixed_back(near, far, weight, query, keys, values, allowed):
    def kernel(
        near_ref,
        far_ref,
        weight_ref,
        query_ref,
        keys_ref,
        values_ref,
        allowed_ref,
        dquery_ref,
        dkv_ref,
        dmixed_ref,
    ):
        dmixed_ref[...] = projected(near_ref, far_ref, weight_ref, True)
        kv = (keys_ref[...], values_ref[...])
        mix_back(query_ref, dmixed_ref, *kv, allowed_ref[...], dquery_ref, dkv_ref)

    return local_call(
        kernel,
        [(query.shape, BF), ((VIS, 2 * HD), F32)],
        [near, far, weight, query, keys, values, allowed],
        "dmixed_back",
        [pltpu.VMEM(query.shape, F32)],
    )


def weight_block(weight_ref, at, transposed):
    return weight_ref[at : at + STEP, :] if transposed else weight_ref[:, at : at + STEP]


def product(rows, weight, transposed):
    width = weight.shape[0] if transposed else weight.shape[1]

    def kernel(rows_ref, weight_ref, out_ref):
        dot = dot_nt if transposed else dot_nn
        for at in range(0, width, STEP):
            block = weight_block(weight_ref, at, transposed)
            out_ref[:, at : at + STEP] = dot(rows_ref[...], block).astype(BF)

    return local_call(kernel, [((HALF, width), BF)], [rows, weight], "product")[0]


def product_sum(rows, weight, arrived, transposed):
    width = arrived.shape[1]

    def kernel(rows_ref, weight_ref, arrived_ref, out_ref):
        dot = dot_nt if transposed else dot_nn
        for at in range(0, width, STEP):
            total = dot(rows_ref[...], weight_block(weight_ref, at, transposed))
            total += arrived_ref[:, at : at + STEP].astype(F32)
            out_ref[:, :, at : at + STEP] = total.reshape(CHIPS, ROWS, STEP).astype(BF)

    return local_call(
        kernel, [((CHIPS, ROWS, width), BF)], [rows, weight, arrived], "product_sum"
    )[0]


def chosen_product(first, rows, in_weight, out_weight):
    width = out_weight.shape[1]

    def kernel(first_ref, rows_ref, in_ref, out_weight_ref, out_ref):
        for transposed, ref in ((True, in_ref), (False, out_weight_ref)):

            @pl.when(first_ref[0] == int(transposed))
            def _():
                dot = dot_nt if transposed else dot_nn
                for at in range(0, width, STEP):
                    block = weight_block(ref, at, transposed)
                    out_ref[:, at : at + STEP] = dot(rows_ref[...], block).astype(BF)

    return chosen_call(
        kernel, ((HALF, width), BF), first, [rows, in_weight, out_weight], "chosen_product"
    )


def chosen_product_sum(first, rows, in_weight, out_weight, arrived):
    width = out_weight.shape[1]

    def kernel(first_ref, rows_ref, in_ref, out_weight_ref, arrived_ref, out_ref):
        for transposed, ref in ((True, in_ref), (False, out_weight_ref)):

            @pl.when(first_ref[0] == int(transposed))
            def _():
                dot = dot_nt if transposed else dot_nn
                for at in range(0, width, STEP):
                    total = dot(rows_ref[...], weight_block(ref, at, transposed))
                    total += arrived_ref[:, at : at + STEP].astype(F32)
                    out_ref[:, :, at : at + STEP] = total.reshape(CHIPS, ROWS, STEP).astype(BF)

    return chosen_call(
        kernel,
        ((CHIPS, ROWS, width), BF),
        first,
        [rows, in_weight, out_weight, arrived],
        "chosen_product_sum",
    )


def chosen_call(kernel, out, first, ins, name):
    held = pl.BlockSpec(memory_space=pltpu.VMEM)
    return pl.pallas_call(
        kernel,
        in_specs=[pl.BlockSpec(memory_space=pltpu.SMEM)] + [held] * len(ins),
        out_specs=held,
        out_shape=jax.ShapeDtypeStruct(*out),
        compiler_params=pltpu.CompilerParams(vmem_limit_bytes=24 * 1024 * 1024),
        name=name,
    )(first.astype(jnp.int32).reshape(1), *ins)


def chips_sum(pieces_ref):
    total = pieces_ref[0].astype(F32)
    for chip in range(1, CHIPS):
        total += pieces_ref[chip].astype(F32)
    return total


def input_grad(upstream_ref, inputs_ref, total):
    back = norm_back(inputs_ref[...].astype(F32), total, 1e-05)
    return (upstream_ref[...].astype(F32) + back).astype(BF)


def grad_rows(pieces, upstream, inputs):
    def kernel(pieces_ref, upstream_ref, inputs_ref, grad_ref):
        grad_ref[...] = input_grad(upstream_ref, inputs_ref, chips_sum(pieces_ref))

    return local_call(kernel, [(inputs.shape, BF)], [pieces, upstream, inputs], "grad_rows")[0]


def last_rows(first, gate_value, pieces, text, upstream, hidden, passed, grad):
    def kernel(
        first_ref,
        gate_ref,
        pieces_ref,
        text_ref,
        upstream_ref,
        hidden_ref,
        passed_ref,
        grad_ref,
        hidden_out_ref,
        grad_out_ref,
    ):
        total = chips_sum(pieces_ref)

        @pl.when(first_ref[0] == 1)
        def _():
            hidden_out_ref[...] = hidden_ref[...]
            grad_out_ref[...] = input_grad(upstream_ref, text_ref, total)

        @pl.when(first_ref[0] == 0)
        def _():
            term = gate_ref[0] * total
            hidden_out_ref[...] = (passed_ref[...].astype(F32) + term).astype(BF)
            grad_out_ref[...] = grad_ref[...]

    scalar = pl.BlockSpec(memory_space=pltpu.SMEM)
    shape = jax.ShapeDtypeStruct(text.shape, BF)
    return pl.pallas_call(
        kernel,
        in_specs=[scalar, scalar] + [pl.BlockSpec()] * 6,
        out_shape=[shape, shape],
        compiler_params=pltpu.CompilerParams(vmem_limit_bytes=24 * 1024 * 1024),
        name="last_rows",
    )(
        first.astype(jnp.int32).reshape(1),
        gate_value.reshape(1),
        pieces,
        text,
        upstream,
        hidden,
        passed,
        grad,
    )


def token_sums(away_product, near_product, rows):
    away = away_product(rows[HALF:])
    return near_product(rows[:HALF], hop(away, TO_CORE))


def kv_product(rows, w_key, w_value, arrived=None):
    def kernel(rows_ref, key_ref, value_ref, *refs):
        out_ref = refs[-1]
        for which, ref in enumerate((key_ref, value_ref)):
            part = dot_nn(rows_ref[...], ref[...])
            lanes = slice(which * HD, which * HD + HD)
            for chip in range(CHIPS):
                head, half = chip // 2, chip % 2
                piece = part[
                    half * TILE_ROWS : (half + 1) * TILE_ROWS, head * HD : (head + 1) * HD
                ]
                if arrived is not None:
                    piece = piece + refs[0][chip, :, lanes].astype(F32)
                out_ref[chip, :, lanes] = piece.astype(BF)

    more = [] if arrived is None else [arrived]
    return local_call(
        kernel,
        [((CHIPS, TILE_ROWS, 2 * HD), BF)],
        [rows, w_key, w_value, *more],
        "kv_product",
    )[0]


def vision_back(near, far, w_key, w_value):
    def kernel(near_ref, far_ref, key_ref, value_ref, out_ref):
        for core, ref in enumerate((near_ref, far_ref)):
            for half in range(2):
                total = 0.0
                for head in range(CHIPS // 2):
                    lanes = slice(head * HD, head * HD + HD)
                    piece = ref[2 * head + half]
                    total += dot_nt(piece[:, :HD], key_ref[:, lanes])
                    total += dot_nt(piece[:, HD:], value_ref[:, lanes])
                out_ref[half, core] = total

    return local_call(
        kernel,
        [((2, 2, TILE_ROWS, w_key.shape[0]), F32)],
        [near, far, w_key, w_value],
        "vision_back",
    )[0]


def weight_back(visions, near, far):
    samples = len(visions)
    heads = near.shape[0] // samples // 2

    def kernel(*refs):
        vision_refs = refs[:samples]
        near_ref, far_ref, key_ref, value_ref = refs[samples:]
        vision = jnp.concatenate([ref[...] for ref in vision_refs], axis=0)
        for head in range(heads):
            pieces = [
                ref[(sample * heads + head) * 2 + half]
                for sample in range(samples)
                for ref in (near_ref, far_ref)
                for half in range(2)
            ]
            total = dot_tn(vision, jnp.concatenate(pieces, axis=0))
            lanes = slice(head * HD, head * HD + HD)
            key_ref[:, lanes] = total[:, :HD]
            value_ref[:, lanes] = total[:, HD:]

    shape = ((visions[0].shape[-1], heads * HD), F32)
    return local_call(kernel, [shape, shape], [*visions, near, far], "weight_back")


def per_device(
    text,
    vision,
    query_weight,
    key_weight,
    value_weight,
    out_weight,
    gate,
    cotangent,
    tile_table,
    vision_tiles,
    text_lengths,
):
    section = lax.axis_index("depth")
    first = section == 0
    tensor = lax.axis_index("tensor")
    core = tensor % 2
    row = tensor // 16
    tile = tensor % 4
    w_key = key_weight[0]
    w_value = value_weight[0]
    gate_value = jnp.tanh(gate[0])
    depth_swap = [(0, 1), (1, 0)]
    text_f = text.astype(F32)
    cotangent_f = cotangent.astype(F32)

    opening = jnp.where(first, normalize(text_f, 1e-05), gate_value * cotangent_f).astype(BF)
    w_query = query_weight[0]
    w_out = out_weight[0]
    opened_near = chip_exchange(jnp.broadcast_to(opening[None], (CHIPS,) + opening.shape))

    place = jnp.arange(SEQ, dtype=jnp.int32)
    side = jnp.bitwise_xor(core, place // HALF)
    row_at = (place % HALF) // ROWS * (2 * ROWS) + side * ROWS + place % ROWS
    tile_ok = jnp.arange(TILES, dtype=jnp.int32) < vision_tiles[0]
    block_ok = ((tile_table[0] > 0) & tile_ok[None, :]).astype(BF)
    in_block = (row_at // TBLK)[:, None] == jnp.arange(SEQ // TBLK, dtype=jnp.int32)[None, :]
    in_block = in_block & (row_at < text_lengths[0])[:, None]
    column_tile = jnp.bitwise_xor(tile, jnp.arange(VIS, dtype=jnp.int32) // TILE_ROWS)
    in_tile = jnp.arange(TILES, dtype=jnp.int32)[:, None] == column_tile[None, :]
    allowed = dot_nn(dot_nn(in_block.astype(BF), block_ok).astype(BF), in_tile.astype(BF))

    other = lax.ppermute(vision, "depth", depth_swap)
    tiles = vision.reshape(2, TILE_ROWS, vision.shape[1])
    other_tiles = other.reshape(2, TILE_ROWS, vision.shape[1])

    def tiles_of(which):
        mine = jnp.where(which == 0, tiles[0], tiles[1])
        theirs = jnp.where(which == 0, other_tiles[0], other_tiles[1])
        return jnp.concatenate(
            [jnp.where(first, mine, theirs), jnp.where(first, theirs, mine)], axis=0
        )

    vision_near = tiles_of(core)
    vision_far = tiles_of(1 - core)
    vision_pair = jnp.concatenate([vision_near, vision_far], axis=0)
    samples = lax.axis_size("dp")

    def sample_hop(value, step):
        pairs = [(at, (at + step) % samples) for at in range(samples)]
        return lax.ppermute(value, "dp", pairs)

    vision_all = [vision_pair] + [sample_hop(vision_pair, step) for step in range(1, samples)]
    arrived = hop(kv_product(vision_far, w_key, w_value), TO_CORE)
    pieces = kv_product(vision_near, w_key, w_value, arrived)
    opened_near, pieces, vision_all = lax.optimization_barrier((opened_near, pieces, vision_all))
    opened = (opened_near, hop(opened_near, TO_CORE))
    query_first = project(*opened, w_query, False)
    pieces = after(chip_exchange(pieces), query_first)
    piece = jnp.sum(pieces.astype(F32), axis=0)
    keys_piece = piece[:, :HD]
    kv_piece = jnp.concatenate([normalize(keys_piece, 1e-06), piece[:, HD:]], axis=1).astype(BF)
    head_kv = jnp.concatenate(
        [kv_piece, hop(kv_piece, TO_CORE), hop(kv_piece, KV_PAIR), hop(kv_piece, KV_BOTH)], axis=0
    )
    keys = head_kv[:, :HD]
    values = head_kv[:, HD:]

    def out_sums(rows):
        return token_sums(
            lambda part: product(part, w_out, False),
            lambda part, arrived: product_sum(part, w_out, arrived, False),
            rows,
        )

    def in_sums(rows):
        return token_sums(
            lambda part: product(part, w_query, True),
            lambda part, arrived: product_sum(part, w_query, arrived, True),
            rows,
        )

    def last_sums(rows):
        return token_sums(
            lambda part: chosen_product(first, part, w_query, w_out),
            lambda part, arrived: chosen_product_sum(first, part, w_query, w_out, arrived),
            rows,
        )

    dmixed_second = project(*opened, w_out, True)
    mixed_first = attend(query_first, keys, values, allowed)
    attended = jnp.sum(chip_exchange(out_sums(mixed_first)).astype(F32), axis=0)
    hidden_first = (text_f + gate_value * attended).astype(BF)

    passed = lax.ppermute(hidden_first, "depth", [(0, 1)])
    passed_f = passed.astype(F32)
    middle = gather_chips(normalize(passed_f, 1e-05).astype(BF))
    query_second, dquery_second, dkv_second = query_back(
        *middle, w_query, dmixed_second, keys, values, allowed
    )
    grad_second = grad_rows(chip_exchange(in_sums(dquery_second)), cotangent, passed)
    mixed_second = attend(query_second, keys, values, allowed)

    upstream = lax.ppermute(grad_second, "depth", [(1, 0)])
    upstream_f = upstream.astype(F32)
    closing = gather_chips((gate_value * upstream_f).astype(BF))
    dquery_first, dkv_first = dmixed_back(*closing, w_out, query_first, keys, values, allowed)

    dkv = jnp.where(first, dkv_first, dkv_second)
    dkv_piece = dkv[:TILE_ROWS]
    for at, pairs in ((3, KV_BOTH), (2, KV_PAIR), (1, TO_CORE)):
        away = dkv[at * TILE_ROWS : (at + 1) * TILE_ROWS].astype(BF)
        dkv_piece = dkv_piece + hop(away, pairs).astype(F32)
    dkv_piece = jnp.concatenate(
        [norm_back(keys_piece, dkv_piece[:, :HD], 1e-06), dkv_piece[:, HD:]], axis=1
    ).astype(BF)
    ring_pieces = ring_exchange(jnp.broadcast_to(dkv_piece[None], (RING,) + dkv_piece.shape))
    last_terms = last_sums(jnp.where(first, dquery_first, mixed_second))
    ring_pieces, last_terms = lax.optimization_barrier((ring_pieces, last_terms))
    other_pieces = hop(ring_pieces, TO_ROW)
    pieces_near = jnp.concatenate(
        [
            jnp.where(row == 0, ring_pieces, other_pieces),
            jnp.where(row == 0, other_pieces, ring_pieces),
        ],
        axis=0,
    )
    pieces_far = hop(pieces_near, TO_CORE)
    sample = lax.axis_index("dp")
    share = CHIPS // samples
    columns = []
    for step in range(samples):
        start = (sample + step) % samples * share
        column = lax.dynamic_slice_in_dim(pieces_near, start, share, 0)
        columns.append(sample_hop(column, step) if step else column)
    columns_near = jnp.concatenate(columns, axis=0)
    columns_far = hop(columns_near, TO_CORE)
    key_grad, value_grad = weight_back(vision_all, columns_near, columns_far)
    dvision = vision_back(pieces_near, pieces_far, w_key, w_value)
    mine = lax.dynamic_index_in_dim(dvision, section, 0, False)
    theirs = lax.dynamic_index_in_dim(dvision, 1 - section, 0, False)
    dvision = mine + lax.ppermute(theirs, "depth", depth_swap)
    dvision = jnp.where(core == 0, dvision, dvision[::-1]).reshape(VIS // 2, vision.shape[1])

    hidden, text_grad = last_rows(
        first,
        gate_value,
        chip_exchange(last_terms),
        text,
        upstream,
        hidden_first,
        passed,
        grad_second,
    )
    return (hidden[None], text_grad[None], dvision, key_grad[None], value_grad[None])


def solution(mesh):
    in_specs = (
        P(("dp", "tensor"), None),
        P(("dp", "depth"), "tensor"),
        P("depth", None, "tensor"),
        P("depth", "tensor", None),
        P("depth", "tensor", None),
        P("depth", "tensor", None),
        P("depth"),
        P(("dp", "tensor"), None),
        P("dp", None, None),
        P("dp"),
        P("dp"),
    )
    out_specs = (
        P("depth", ("dp", "tensor"), None),
        P("depth", ("dp", "tensor"), None),
        P(("dp", "depth"), "tensor"),
        P("depth", "tensor", "dp"),
        P("depth", "tensor", "dp"),
    )
    return jax.shard_map(
        per_device, mesh=mesh, in_specs=in_specs, out_specs=out_specs, check_vma=False
    )
```
